32 devices in a mesh: comp: 4 (over y, x), samp: 8 (over z, core).
Axes of the slice: x: 2, y: 2, z: 4, core: 2. Of those that a mesh axis runs over, the one named last changes fastest.
Arguments:
- samples: float32 [2048, 32768], P('comp', 'samp'), may hold values from -1.7 to 1.7
- unmixing: float32 [2048, 2048], P('comp', 'samp'), may hold values from -0.37565048 to 0.37565048, as said below
Outputs:
- decorrelated: float32 [2048, 2048], P('comp', 'samp')
The draws below stay inside these ranges and needn't reach their ends.
Inputs may be any that keep to these rules, and one draw needn't show every extreme that they name: `unmixing`: every entry's magnitude is at most 17 / sqrt(2048).
All inputs are finite; a program needn't handle non-finite values.
Results may differ from the reference program's by a relative error of at most 0.00011.
Values sent between devices are 32-bit elements; how exact they have to be, the bound alone decides.
No kernel may reach another device: no remote copies, remote signals or barrier semaphores. Data moves between devices by JAX's collectives and lax.ppermute only.
A program may use at most 128 MiB of HBM per device.

```python
import jax
import jax.numpy as jnp
from jax import lax

C = 2048
NS_STEPS = 3
SAMPLES = 32768


def draw_unmixing(key, part):
    key_entries = jax.random.fold_in(key, 11)
    key_jitter = jax.random.fold_in(key, 23)
    rows = jnp.arange(C, dtype=jnp.float32) / C
    jitter = jnp.exp(jax.random.uniform(key_jitter, (C,), jnp.float32, jnp.log(0.7), jnp.log(1.4)))
    entries = jnp.clip(jax.random.normal(key_entries, (C, C), jnp.float32), -4.0, 4.0)
    scales = 0.3 * jnp.exp(rows * jnp.log(10.0)) * jitter
    return (entries * scales[:, None] / jnp.sqrt(jnp.float32(C))).astype(jnp.float32)


def steps_of(own_key, extent, cuts, least, top_value):
    def one(position, parts):
        steps = jax.random.uniform(jax.random.fold_in(jax.random.fold_in(own_key, 6), position), (parts,), jnp.float32, least / len(cuts), top_value / len(cuts))
        return jnp.repeat(jnp.exp(steps), extent[position] // parts).reshape((-1,) + (1,) * (len(extent) - position - 1))

    gain = one(*cuts[0])
    for cut in cuts[1:]:
        gain = gain * one(*cut)
    return gain


def setup_inputs(seed: int = 0) -> dict:
    streams_of = jax.random.split(jax.random.key(seed), 3)
    return {
        "samples": jnp.clip(jax.random.uniform(streams_of[0], (C, SAMPLES), jnp.float32, -1.7, 1.7) * steps_of(streams_of[0], (C, SAMPLES), ((0, 4), (1, 8)), -0.4, 0.0), -1.7, 1.7),
        "unmixing": draw_unmixing(jax.random.fold_in(streams_of[2], 71), 0),
    }


highest = lax.Precision.HIGHEST

def reference(samples, unmixing):
    projected = jnp.dot(unmixing, samples, precision=highest)
    contrast = jnp.tanh(projected)
    moment = lax.dot_general(contrast, samples, (((1,), (1,)), ((), ())), precision=highest) / SAMPLES
    slope = lax.optimization_barrier(jnp.sum(1.0 - contrast * contrast, axis=1)) / SAMPLES
    updated = moment - slope[:, None] * unmixing
    scale = 2.5 * jnp.sqrt(jnp.sum(updated * updated) / C + 1e-06)
    current = updated / scale
    for step in range(NS_STEPS):
        gram = lax.dot_general(current, current, (((1,), (1,)), ((), ())), precision=highest)
        current = 1.5 * current - 0.5 * jnp.dot(gram, current, precision=highest)
    return current * jnp.sqrt(jnp.float32(C))
```

```python
import jax
import jax.numpy as jnp
from jax import lax
from jax.sharding import PartitionSpec as P

NS_STEPS = 3
AXES = ("comp", "samp")
CHUNKS = 4
PREC = lax.Precision.HIGH


def matmul(a, b):
    return jnp.dot(a, b, precision=PREC)


def matmul_nt(a, b):
    return lax.dot_general(a, b, (((1,), (1,)), ((), ())), precision=PREC)


def on_device(samples, unmixing):
    n_c, n_s = lax.axis_size("comp"), lax.axis_size("samp")
    c, s = lax.axis_index("comp"), lax.axis_index("samp")
    x, core, z = c % 2, s % 2, s // 2
    z_bits = [1 << i for i in range((n_s // 2).bit_length() - 1)]
    rows, n_local = samples.shape
    width = unmixing.shape[1]
    order = width * n_s
    count = n_local * n_s
    blocks = range(n_c)

    def swap(value, comp_bits=0, samp_bits=0):
        pairs = [
            (i * n_s + j, (i ^ comp_bits) * n_s + (j ^ samp_bits))
            for i in range(n_c)
            for j in range(n_s)
        ]
        return lax.ppermute(value, AXES, pairs)

    half = n_local // 2
    kept = lax.dynamic_slice_in_dim(samples, x * half, half, 1)
    beside = swap(lax.dynamic_slice_in_dim(samples, (1 - x) * half, half, 1), comp_bits=1)
    step = half // CHUNKS
    far = {r: swap(kept, comp_bits=r) for r in range(2, n_c, 2)}

    both = jnp.concatenate([unmixing, swap(unmixing, comp_bits=1)], axis=0)
    weights = lax.all_gather(both, "samp", axis=1, tiled=True)
    parts = [lax.dynamic_slice_in_dim(weights, (c ^ r) * rows, rows, 1) for r in blocks]

    moment = [None] * n_c
    slope = 0.0
    for j in range(CHUNKS):
        cut = slice(j * step, (j + 1) * step)
        beside_cut = beside[:, cut]
        pieces = [kept[:, cut], beside_cut]
        for r in range(2, n_c, 2):
            pieces += [far[r][:, cut], swap(beside_cut, comp_bits=r)]
        projected = sum(matmul(parts[r], pieces[r]) for r in blocks)
        contrast = jnp.tanh(projected)
        slope = slope + jnp.sum(1.0 - contrast * contrast, axis=1)
        for r in blocks:
            term = matmul_nt(contrast, pieces[r])
            moment[r] = term if j == 0 else moment[r] + term

    slope = slope.reshape(2, rows)
    slope = slope + swap(slope, samp_bits=1)
    slope = slope + swap(slope, comp_bits=1)[::-1]
    for bit in z_bits:
        slope = slope + swap(slope, samp_bits=2 * bit)

    def halve(value, axis, bit, samp_bits):
        size = value.shape[axis] // 2
        mine = lax.dynamic_slice_in_dim(value, bit * size, size, axis)
        sent = lax.dynamic_slice_in_dim(value, (1 - bit) * size, size, axis)
        return mine + swap(sent, samp_bits=samp_bits)

    def halve_core(m):
        return [halve(v, v.ndim - 2, core, 1) for v in m]

    def halve_comp(m):
        got = [swap(v[1], comp_bits=1) for v in m]
        return [v[0] + got[i ^ 1] for i, v in enumerate(m)]

    def halve_z(m, bit):
        return [halve(v, v.ndim - 2, (z // bit) % 2, 2 * bit) for v in m]

    moment = halve_core([m.reshape(2, rows, rows) for m in moment])
    front, back = moment[: n_c // 2], moment[n_c // 2 :]
    front = halve_comp(front)
    back = halve_z(back, z_bits[0])
    front = halve_z(front, z_bits[0])
    back = halve_comp(back)
    for bit in z_bits[1:]:
        front, back = halve_z(front, bit), halve_z(back, bit)
    moment = front + back

    size = moment[0].shape[0]
    start = core * (rows // 2)
    span = rows // 2
    for bit in z_bits:
        span = span // 2
        start = start + ((z // bit) % 2) * span
    own_slope = lax.dynamic_slice_in_dim(slope[0], start, size, 0) / count
    own_rows = [lax.dynamic_slice(p, (start, 0), (size, rows)) for p in parts]
    updated = jnp.concatenate(
        [m / count - own_slope[:, None] * w for m, w in zip(moment, own_rows)], axis=1
    )

    for bit in reversed(z_bits):
        other = swap(updated, samp_bits=2 * bit)
        side = (z // bit) % 2
        updated = jnp.where(
            side == 0,
            jnp.concatenate([updated, other], axis=0),
            jnp.concatenate([other, updated], axis=0),
        )

    def seen_from(value, r):
        cols = [value[:, i * rows : (i + 1) * rows] for i in blocks]
        return jnp.concatenate([cols[i ^ r] for i in blocks], axis=1)

    halves = [updated]
    for r in range(1, n_c):
        halves.append(seen_from(swap(updated, comp_bits=r), r))
    mine = jnp.stack(halves)
    other = swap(mine, samp_bits=1)
    whole = jnp.stack([mine, other], axis=1).reshape(order, order)

    gram = matmul_nt(whole, whole)
    scale = 2.5 * jnp.sqrt(jnp.sum(whole * whole) / order + 1e-06)
    gram = gram / (scale * scale)
    share = width // n_c
    first = s * width + c * share
    column = ((first // rows) ^ c) * rows + first % rows
    current = lax.dynamic_slice_in_dim(whole, column, share, 1) / scale

    def gram_times(value, level):
        if level == 0:
            return matmul(gram, value)
        for _ in range(2):
            value = advance(value, level - 1)
        return gram_times(value, level - 1)

    def advance(value, level):
        return 1.5 * value - 0.5 * gram_times(value, level)

    for level in range(NS_STEPS):
        current = advance(current, level)
    current = current * jnp.sqrt(jnp.float32(order))

    current = current.reshape(n_c, 2, rows // 2, share)
    current = jnp.where(core == 0, current, current[:, ::-1]).reshape(n_c, rows, share)
    got = [current[0]] + [swap(current[r], comp_bits=r) for r in range(1, n_c)]
    bit = 1
    while bit < n_c:
        got = [jnp.where((c // bit) % 2 == 0, got[i], got[i ^ bit]) for i in blocks]
        bit *= 2
    return jnp.concatenate(got, axis=1)


def solution(mesh):
    return jax.shard_map(
        on_device,
        mesh=mesh,
        in_specs=(P("comp", "samp"), P("comp", "samp")),
        out_specs=P("comp", "samp"),
        check_vma=False,
    )
```

```python
import functools

import jax
import jax.numpy as jnp
from jax import lax
from jax.experimental import pallas as pl
from jax.experimental.pallas import tpu as pltpu
from jax.sharding import PartitionSpec as P

NS_STEPS = 3
AXES = ("comp", "samp")
FRACTIONS = (4, 4, 4, 8, 8)
LANES = 128
VMEM_BYTES = 60 * 2**20
f32, bf16 = jnp.float32, jnp.bfloat16


def split(v):
    hi = v.astype(bf16)
    return hi, (v - hi.astype(f32)).astype(bf16)


def dot(a, b):
    return jnp.dot(a, b, preferred_element_type=f32)


def dot_nt(a, b):
    return lax.dot_general(a, b, (((1,), (1,)), ((), ())), preferred_element_type=f32)


def weights_kernel(n_z, *refs):
    pieces, (wh, wl) = refs[:-2], refs[-2:]
    s = lax.axis_index("samp")
    z, core = s // 2, s % 2
    rows, width = pieces[0].shape
    i = 0
    for r in range(2):
        for dz in range(n_z):
            for dk in range(2):
                hi, lo = split(pieces[i][...])
                col = pl.multiple_of(((z ^ dz) * 2 + (core ^ dk)) * width, width)
                wh[r * rows : (r + 1) * rows, pl.ds(col, width)] = hi
                wl[r * rows : (r + 1) * rows, pl.ds(col, width)] = lo
                i += 1


def assemble_weights(pieces, n_z):
    rows, width = pieces[0].shape
    shape = jax.ShapeDtypeStruct((2 * rows, 2 * n_z * width), bf16)
    return pl.pallas_call(
        functools.partial(weights_kernel, n_z),
        out_shape=(shape, shape),
        in_specs=[pl.BlockSpec(memory_space=pltpu.VMEM)] * len(pieces),
        out_specs=(pl.BlockSpec(memory_space=pltpu.VMEM),) * 2,
        compiler_params=pltpu.CompilerParams(vmem_limit_bytes=VMEM_BYTES),
        cost_estimate=pl.CostEstimate(
            flops=4 * rows * width * len(pieces),
            transcendentals=0,
            bytes_accessed=8 * rows * width * len(pieces),
        ),
    )(*pieces)


def moment_kernel(first, n_c, *refs):
    pieces, refs = refs[:n_c], refs[n_c:]
    if first:
        wh, wl, m_out, s_out, xh, xl = refs
    else:
        wh, wl, m_in, s_in, m_out, s_out, xh, xl = refs
    rows = pieces[0].shape[0]
    c = lax.axis_index("comp")

    @pl.when(pl.program_id(0) == 0)
    def _():
        for r, piece in enumerate(pieces):
            hi, lo = split(piece[...])
            place = pl.ds(pl.multiple_of((c ^ r) * rows, rows), rows)
            xh[place, :] = hi
            xl[place, :] = lo

    t = jnp.tanh(dot(wh[...], xh[...]) + dot(wh[...], xl[...]) + dot(wl[...], xh[...]))
    d = 1.0 - t * t
    part = d[:, :LANES]
    for q in range(1, d.shape[1] // LANES):
        part = part + d[:, q * LANES : (q + 1) * LANES]
    s_out[...] = part if first else s_in[...] + part
    th, tl = split(t)
    m = dot_nt(th, xh[...]) + dot_nt(th, xl[...]) + dot_nt(tl, xh[...])
    m_out[...] = m if first else m_in[...] + m


def moment_chunk(pieces, offsets, size, wh, wl, state):
    n_rows, order = wh.shape
    rows = pieces[0].shape[0]
    block = n_rows // 4
    first = state is None
    carried = [] if first else list(state)
    n_c = len(pieces)

    def by_rows(n):
        return pl.BlockSpec((block, n), lambda i: (i, 0))

    def at(j):
        return pl.BlockSpec((rows, size), lambda i: (0, j), pipeline_mode=pl.Buffered(1))

    return pl.pallas_call(
        functools.partial(moment_kernel, first, n_c),
        grid=(n_rows // block,),
        out_shape=(
            jax.ShapeDtypeStruct((n_rows, order), f32),
            jax.ShapeDtypeStruct((n_rows, LANES), f32),
        ),
        in_specs=[at(j) for j in offsets]
        + [by_rows(order)] * 2
        + ([] if first else [by_rows(order), by_rows(LANES)]),
        out_specs=(by_rows(order), by_rows(LANES)),
        scratch_shapes=[pltpu.VMEM((order, size), bf16)] * 2,
        input_output_aliases={} if first else {n_c + 2: 0, n_c + 3: 1},
        compiler_params=pltpu.CompilerParams(
            vmem_limit_bytes=VMEM_BYTES, dimension_semantics=("arbitrary",)
        ),
        cost_estimate=pl.CostEstimate(
            flops=12 * n_rows * order * size,
            transcendentals=n_rows * size,
            bytes_accessed=4 * order * size + 12 * n_rows * order,
        ),
    )(*pieces, wh, wl, *carried)


def schedule(steps):
    products = []

    def advance(level, src, held):
        held = held | {src}
        inner = src
        for k in reversed(range(level)):
            for _ in range(2):
                inner = advance(k, inner, held)
        into = min(set(range(8)) - held - {inner})
        products.append((into, inner, src))
        return into

    value = 0
    for level in range(steps):
        value = advance(level, value, frozenset())
    return products, value


def newton_kernel(last, block, rows, places, n_in, *refs):
    table, pieces, out_ref = refs[0], refs[1 : n_in + 1], refs[n_in + 1]
    stage, uh, ul, gh, gl, rhs, vectors, squares, sem = refs[n_in + 2 :]
    order = uh.shape[0]
    tall, lanes = rhs.shape[0], rhs.shape[0] // 2
    size = pieces[0].shape[0]
    n = order // block
    c, s = lax.axis_index("comp"), lax.axis_index("samp")
    z, core = s // 2, s % 2
    first = (s * (lax.axis_size("comp") * lanes)) + c * lanes
    aligned = pl.multiple_of(first // LANES * LANES, LANES)
    shift = lax.rem(LANES - (first - aligned), LANES)
    slots = stage.shape[0]

    def copy(i):
        return pltpu.make_async_copy(pieces[i], stage.at[i % slots], sem.at[i % slots])

    for i in range(slots - 1):
        copy(i).start()
    squares[...] = jnp.zeros_like(squares)
    for i in range(n_in):
        if i + slots - 1 < n_in:
            copy(i + slots - 1).start()
        copy(i).wait()
        r, dz, dk = places[i]
        start = (core ^ dk) * (rows // 2)
        span, bit = rows // 2, 1
        while span > size:
            span //= 2
            start = start + (((z ^ dz) // bit) % 2) * span
            bit *= 2
        start = r * rows + start

        @pl.loop(0, size // 16)
        def _(q):
            here = pl.ds(pl.multiple_of(start + q * 16, 16), 16)
            v = stage[i % slots, pl.ds(pl.multiple_of(q * 16, 16), 16), :]
            part = v * v
            total = part[:, :LANES]
            for t in range(1, order // LANES):
                total = total + part[:, t * LANES : (t + 1) * LANES]
            squares[...] += total
            hi, lo = split(v)
            uh[here, :] = hi
            ul[here, :] = lo

    @pl.loop(0, order // block)
    def _(b):
        here = pl.ds(pl.multiple_of(b * block, block), block)
        cols = pl.ds(aligned, LANES)
        v = uh[here, cols].astype(f32) + ul[here, cols].astype(f32)
        v = pltpu.roll(v, shift, 1).T[:lanes]
        vectors[0, :lanes, here] = v
        vectors[0, lanes:, here] = v

    @pl.loop(0, n)
    def _(i):
        here = pl.ds(pl.multiple_of(i * block, block), block)

        @pl.loop(0, i + 1)
        def _(j):
            there = pl.ds(pl.multiple_of(j * block, block), block)
            g = dot_nt(uh[here, :], uh[there, :])
            g += dot_nt(uh[here, :], ul[there, :])
            g += dot_nt(ul[here, :], uh[there, :])
            hi, lo = split(g)
            gh[here, there] = hi
            gl[here, there] = lo

            @pl.when(j < i)
            def _():
                hi, lo = split(g.T)
                gh[there, here] = hi
                gl[there, here] = lo

    scale2 = 6.25 * (jnp.sum(squares[...]) / order + 1e-06)
    upper = lax.broadcasted_iota(jnp.int32, (tall, order), 0) < lanes
    tile = order // 2

    @pl.loop(0, table.shape[0] // 3)
    def _(p):
        into, src, base = table[3 * p], table[3 * p + 1], table[3 * p + 2]
        hi, lo = split(vectors[src])
        rhs[...] = jnp.where(upper, hi, lo)

        @pl.loop(0, order // tile)
        def _(b):
            cols = pl.ds(pl.multiple_of(b * tile, tile), tile)
            e = dot(rhs[...], gh[:, cols]) + dot(rhs[...], gl[:, cols])
            e = e + jnp.concatenate([e[lanes:], e[:lanes]], axis=0)
            vectors[into, :, cols] = 1.5 * vectors[base, :, cols] - (0.5 / scale2) * e

    out_ref[...] = vectors[last, :lanes] * (jnp.sqrt(jnp.float32(order)) / jnp.sqrt(scale2))


def newton(pieces, places, rows, share):
    size, order = pieces[0].shape
    block = min(256, order)
    square = pltpu.VMEM((order, order), bf16)
    products, last = schedule(NS_STEPS)
    n_buffers = 1 + max(into for into, _, _ in products)
    table = jnp.array([i for p in products for i in p], jnp.int32)
    return pl.pallas_call(
        functools.partial(newton_kernel, last, block, rows, places, len(pieces)),
        out_shape=jax.ShapeDtypeStruct((share, order), f32),
        in_specs=[pl.BlockSpec(memory_space=pltpu.SMEM)]
        + [pl.BlockSpec(memory_space=pl.ANY)] * len(pieces),
        out_specs=pl.BlockSpec(memory_space=pltpu.VMEM),
        scratch_shapes=[pltpu.VMEM((4, size, order), f32)]
        + [square] * 4
        + [
            pltpu.VMEM((2 * share, order), bf16),
            pltpu.VMEM((n_buffers, 2 * share, order), f32),
            pltpu.VMEM((16, LANES), f32),
            pltpu.SemaphoreType.DMA((4,)),
        ],
        compiler_params=pltpu.CompilerParams(vmem_limit_bytes=VMEM_BYTES),
    )(table, *pieces)


def on_device(samples, unmixing):
    n_c, n_s = lax.axis_size("comp"), lax.axis_size("samp")
    c, s = lax.axis_index("comp"), lax.axis_index("samp")
    x, core, z = c % 2, s % 2, s // 2
    n_z = n_s // 2
    z_bits = [1 << i for i in range(n_z.bit_length() - 1)]
    rows, n_local = samples.shape
    width = unmixing.shape[1]
    order = width * n_s
    count = n_local * n_s
    share = width // n_c

    def swap(value, comp_bits=0, samp_bits=0):
        pairs = [
            (i * n_s + j, (i ^ comp_bits) * n_s + (j ^ samp_bits))
            for i in range(n_c)
            for j in range(n_s)
        ]
        return lax.ppermute(value, AXES, pairs)

    half = n_local // 2
    beside = swap(lax.dynamic_slice_in_dim(samples, (1 - x) * half, half, 1), comp_bits=1)
    kept = lax.dynamic_slice_in_dim(samples, x * half, half, 1)
    far = {r: swap(kept, comp_bits=r) for r in range(2, n_c, 2)}

    def gather_z(piece, bits):
        found = {0: piece}
        for bit in bits:
            found |= {dz ^ bit: swap(p, samp_bits=2 * bit) for dz, p in found.items()}
        return [found[dz] for dz in range(n_z)]

    near = gather_z(unmixing, z_bits)
    next_to = gather_z(swap(unmixing, comp_bits=1), z_bits[::-1])
    w_pieces = [p for q in near + next_to for p in (q, swap(q, samp_bits=1))]
    wh, wl = assemble_weights(w_pieces, n_z)

    state, start = None, 0
    for fraction in FRACTIONS:
        size = half // fraction
        cut, j = slice(start, start + size), start // size
        pieces, offsets = [kept, beside], [j, j]
        for r in range(2, n_c, 2):
            pieces += [far[r], swap(beside[:, cut], comp_bits=r)]
            offsets += [j, 0]
        state = moment_chunk(pieces, offsets, size, wh, wl, state)
        start += size
    moment, slope = state

    slope = jnp.sum(slope, axis=1).reshape(2, rows)
    slope = slope + swap(slope, samp_bits=1)
    slope = slope + swap(slope, comp_bits=1)[::-1]
    for bit in z_bits:
        slope = slope + swap(slope, samp_bits=2 * bit)

    def halve(value, bit, samp_bits):
        axis = value.ndim - 2
        size = value.shape[axis] // 2
        mine = lax.dynamic_slice_in_dim(value, bit * size, size, axis)
        sent = lax.dynamic_slice_in_dim(value, (1 - bit) * size, size, axis)
        return mine + swap(sent, samp_bits=samp_bits)

    def halve_comp(value):
        return value[0] + swap(value[1], comp_bits=1)

    def halve_z(value, bit):
        return halve(value, (z // bit) % 2, 2 * bit)

    moment = moment.reshape(2, rows, order)
    front = halve(moment[:, :, : order // 2], core, 1)
    back = halve(moment[:, :, order // 2 :], core, 1)
    front, back = halve_comp(front), halve_z(back, z_bits[0])
    front, back = halve_z(front, z_bits[0]), halve_comp(back)
    for bit in z_bits[1:]:
        front, back = halve_z(front, bit), halve_z(back, bit)
    moment = jnp.concatenate([front, back], axis=1)

    size = moment.shape[0]
    start, span = core * (rows // 2), rows // 2
    for bit in z_bits:
        span //= 2
        start = start + ((z // bit) % 2) * span
    own_slope = lax.dynamic_slice_in_dim(slope[0], start, size, 0) / count
    parts = [None] * n_s
    for dz in range(n_z):
        for dk in range(2):
            parts[dz * 2 + dk] = lax.dynamic_slice_in_dim(w_pieces[dz * 2 + dk], start, size, 0)
    own_rows = jnp.stack(parts)
    for bit in [2 * b for b in z_bits] + [1]:
        turned = jnp.stack([own_rows[i ^ bit] for i in range(n_s)])
        own_rows = jnp.where((s // bit) % 2 == 0, own_rows, turned)
    own_rows = own_rows.transpose(1, 0, 2).reshape(size, order)
    updated = moment / count - own_slope[:, None] * own_rows

    pieces, places = [], []
    for dz, piece in enumerate(gather_z(updated, z_bits)):
        found = {0: piece}
        bits = [1 << i for i in range(n_c.bit_length() - 1)]
        for bit in bits if dz % 2 else bits[::-1]:
            found |= {r ^ bit: swap(p, comp_bits=bit) for r, p in found.items()}
        for r, p in found.items():
            pieces += [p, swap(p, samp_bits=1)]
            places += [(r, dz, 0), (r, dz, 1)]

    current = newton(pieces, tuple(places), rows, share)

    got = [current[:, :rows]]
    got += [swap(current[:, r * rows : (r + 1) * rows], comp_bits=r) for r in range(1, n_c)]
    bit = 1
    while bit < n_c:
        got = [jnp.where((c // bit) % 2 == 0, got[i], got[i ^ bit]) for i in range(n_c)]
        bit *= 2
    return jnp.concatenate(got, axis=0).T


def solution(mesh):
    return jax.shard_map(
        on_device,
        mesh=mesh,
        in_specs=(P("comp", "samp"), P("comp", "samp")),
        out_specs=P("comp", "samp"),
        check_vma=False,
    )
```

```python
import functools

import jax
import jax.numpy as jnp
from jax import lax
from jax.experimental import pallas as pl
from jax.experimental.pallas import tpu as pltpu
from jax.sharding import PartitionSpec as P


NS_STEPS = 3
AXES = ("comp", "samp")
CHUNKS = 4
BLOCKS = 2
LANES = 128
VMEM_BYTES = 60 * 2**20
f32, bf16 = jnp.float32, jnp.bfloat16


def split(v):
    hi = v.astype(bf16)
    return hi, (v - hi.astype(f32)).astype(bf16)


def dot(a, b):
    return jnp.dot(a, b, preferred_element_type=f32)


def dot_nt(a, b):
    return lax.dot_general(a, b, (((1,), (1,)), ((), ())), preferred_element_type=f32)


def weights_kernel(n_z, *refs):
    pieces, (wh, wl) = refs[:-2], refs[-2:]
    z = lax.axis_index("samp") // 2
    rows, width = pieces[0].shape
    for r in range(2):
        for dz in range(n_z):
            hi, lo = split(pieces[r * n_z + dz][...])
            col = pl.multiple_of((z ^ dz) * width, width)
            wh[r * rows : (r + 1) * rows, pl.ds(col, width)] = hi
            wl[r * rows : (r + 1) * rows, pl.ds(col, width)] = lo


def assemble_weights(pieces, n_z):
    rows, width = pieces[0].shape
    shape = jax.ShapeDtypeStruct((2 * rows, n_z * width), bf16)
    return pl.pallas_call(
        functools.partial(weights_kernel, n_z),
        out_shape=(shape, shape),
        in_specs=[pl.BlockSpec(memory_space=pltpu.VMEM)] * len(pieces),
        out_specs=(pl.BlockSpec(memory_space=pltpu.VMEM),) * 2,
        compiler_params=pltpu.CompilerParams(vmem_limit_bytes=VMEM_BYTES),
        cost_estimate=pl.CostEstimate(
            flops=4 * rows * width * len(pieces),
            transcendentals=0,
            bytes_accessed=8 * rows * width * len(pieces),
        ),
    )(*pieces)


def moment_kernel(first, n_p, *refs):
    pieces, refs = refs[:n_p], refs[n_p:]
    if first:
        wh, wl, m_out, s_out, xh, xl = refs
    else:
        wh, wl, m_in, s_in, m_out, s_out, xh, xl = refs
    rows, size = pieces[0].shape
    c = lax.axis_index("comp")

    @pl.when(pl.program_id(0) == 0)
    def _():
        for i, piece in enumerate(pieces):
            hi, lo = split(piece[...])
            place = pl.ds(pl.multiple_of((c ^ (i // 2)) * rows, rows), rows)
            cols = slice(i % 2 * size, (i % 2 + 1) * size)
            xh[place, cols] = hi
            xl[place, cols] = lo

    t = jnp.tanh(dot(wh[...], xh[...]) + dot(wh[...], xl[...]) + dot(wl[...], xh[...]))
    d = 1.0 - t * t
    part = d[:, :LANES]
    for q in range(1, d.shape[1] // LANES):
        part = part + d[:, q * LANES : (q + 1) * LANES]
    s_out[...] = part if first else s_in[...] + part
    th, tl = split(t)
    m = dot_nt(th, xh[...]) + dot_nt(th, xl[...]) + dot_nt(tl, xh[...])
    m_out[...] = m if first else m_in[...] + m


def moment_chunk(pieces, wh, wl, state):
    n_rows, order = wh.shape
    rows, size = pieces[0].shape
    block = n_rows // BLOCKS
    first = state is None
    carried = [] if first else list(state)
    n_p = len(pieces)

    def by_rows(n):
        return pl.BlockSpec((block, n), lambda i: (i, 0))

    once = pl.BlockSpec((rows, size), lambda i: (0, 0), pipeline_mode=pl.Buffered(1))
    return pl.pallas_call(
        functools.partial(moment_kernel, first, n_p),
        grid=(BLOCKS,),
        out_shape=(
            jax.ShapeDtypeStruct((n_rows, order), f32),
            jax.ShapeDtypeStruct((n_rows, LANES), f32),
        ),
        in_specs=[once] * n_p
        + [by_rows(order)] * 2
        + ([] if first else [by_rows(order), by_rows(LANES)]),
        out_specs=(by_rows(order), by_rows(LANES)),
        scratch_shapes=[pltpu.VMEM((order, 2 * size), bf16)] * 2,
        input_output_aliases={} if first else {n_p + 2: 0, n_p + 3: 1},
        compiler_params=pltpu.CompilerParams(
            vmem_limit_bytes=VMEM_BYTES, dimension_semantics=("arbitrary",)
        ),
        cost_estimate=pl.CostEstimate(
            flops=24 * n_rows * order * size,
            transcendentals=2 * n_rows * size,
            bytes_accessed=8 * order * size + 12 * n_rows * order,
        ),
    )(*pieces, wh, wl, *carried)


def schedule(steps):
    products = []

    def advance(level, src, held):
        held = held | {src}
        inner = src
        for k in reversed(range(level)):
            for _ in range(2):
                inner = advance(k, inner, held)
        into = min(set(range(8)) - held - {inner})
        products.append((into, inner, src))
        return into

    value = 0
    for level in range(steps):
        value = advance(level, value, frozenset())
    return products, value


def newton_kernel(last, block, rows, places, n_in, *refs):
    table, pieces, out_ref = refs[0], refs[1 : n_in + 1], refs[n_in + 1]
    stage, uh, ul, gh, gl, rhs, vectors, squares, sem = refs[n_in + 2 :]
    order = uh.shape[0]
    tall, lanes = rhs.shape[0], rhs.shape[0] // 2
    size = pieces[0].shape[0]
    n = order // block
    c, s = lax.axis_index("comp"), lax.axis_index("samp")
    z, core = s // 2, s % 2
    first = (s * (lax.axis_size("comp") * lanes)) + c * lanes
    aligned = pl.multiple_of(first // LANES * LANES, LANES)
    shift = lax.rem(LANES - (first - aligned), LANES)
    slots = stage.shape[0]

    def copy(i):
        return pltpu.make_async_copy(pieces[i], stage.at[i % slots], sem.at[i % slots])

    for i in range(slots - 1):
        copy(i).start()
    squares[...] = jnp.zeros_like(squares)
    for i in range(n_in):
        if i + slots - 1 < n_in:
            copy(i + slots - 1).start()
        copy(i).wait()
        r, dz, dk = places[i]
        start = (core ^ dk) * (rows // 2)
        span, bit = rows // 2, 1
        while span > size:
            span //= 2
            start = start + (((z ^ dz) // bit) % 2) * span
            bit *= 2
        start = r * rows + start

        @pl.loop(0, size // 16)
        def _(q):
            here = pl.ds(pl.multiple_of(start + q * 16, 16), 16)
            v = stage[i % slots, pl.ds(pl.multiple_of(q * 16, 16), 16), :]
            part = v * v
            total = part[:, :LANES]
            for t in range(1, order // LANES):
                total = total + part[:, t * LANES : (t + 1) * LANES]
            squares[...] += total
            hi, lo = split(v)
            uh[here, :] = hi
            ul[here, :] = lo

    @pl.loop(0, order // block)
    def _(b):
        here = pl.ds(pl.multiple_of(b * block, block), block)
        cols = pl.ds(aligned, LANES)
        v = uh[here, cols].astype(f32) + ul[here, cols].astype(f32)
        v = pltpu.roll(v, shift, 1).T[:lanes]
        vectors[0, :lanes, here] = v
        vectors[0, lanes:, here] = v

    @pl.loop(0, n)
    def _(i):
        here = pl.ds(pl.multiple_of(i * block, block), block)

        @pl.loop(0, i + 1)
        def _(j):
            there = pl.ds(pl.multiple_of(j * block, block), block)
            g = dot_nt(uh[here, :], uh[there, :])
            g += dot_nt(uh[here, :], ul[there, :])
            g += dot_nt(ul[here, :], uh[there, :])
            hi, lo = split(g)
            gh[here, there] = hi
            gl[here, there] = lo

            @pl.when(j < i)
            def _():
                hi, lo = split(g.T)
                gh[there, here] = hi
                gl[there, here] = lo

    scale2 = 6.25 * (jnp.sum(squares[...]) / order + 1e-06)
    upper = lax.broadcasted_iota(jnp.int32, (tall, order), 0) < lanes
    tile = order // 2

    @pl.loop(0, table.shape[0] // 3)
    def _(p):
        into, src, base = table[3 * p], table[3 * p + 1], table[3 * p + 2]
        hi, lo = split(vectors[src])
        rhs[...] = jnp.where(upper, hi, lo)

        @pl.loop(0, order // tile)
        def _(b):
            cols = pl.ds(pl.multiple_of(b * tile, tile), tile)
            e = dot(rhs[...], gh[:, cols]) + dot(rhs[...], gl[:, cols])
            e = e + jnp.concatenate([e[lanes:], e[:lanes]], axis=0)
            vectors[into, :, cols] = 1.5 * vectors[base, :, cols] - (0.5 / scale2) * e

    out_ref[...] = vectors[last, :lanes] * (jnp.sqrt(jnp.float32(order)) / jnp.sqrt(scale2))


def newton(pieces, places, rows, share):
    size, order = pieces[0].shape
    block = min(256, order)
    square = pltpu.VMEM((order, order), bf16)
    products, last = schedule(NS_STEPS)
    n_buffers = 1 + max(into for into, _, _ in products)
    table = jnp.array([i for p in products for i in p], jnp.int32)
    return pl.pallas_call(
        functools.partial(newton_kernel, last, block, rows, places, len(pieces)),
        out_shape=jax.ShapeDtypeStruct((share, order), f32),
        in_specs=[pl.BlockSpec(memory_space=pltpu.SMEM)]
        + [pl.BlockSpec(memory_space=pl.ANY)] * len(pieces),
        out_specs=pl.BlockSpec(memory_space=pltpu.VMEM),
        scratch_shapes=[pltpu.VMEM((4, size, order), f32)]
        + [square] * 4
        + [
            pltpu.VMEM((2 * share, order), bf16),
            pltpu.VMEM((n_buffers, 2 * share, order), f32),
            pltpu.VMEM((16, LANES), f32),
            pltpu.SemaphoreType.DMA((4,)),
        ],
        compiler_params=pltpu.CompilerParams(vmem_limit_bytes=VMEM_BYTES),
    )(table, *pieces)


def spread(n_z, n_c):
    every = [(dz, r) for dz in range(n_z) for r in range(n_c)]
    return sorted(every, key=lambda p: (p[0].bit_count() + p[1].bit_count(), p[1], p[0]))


def on_device(samples, unmixing):
    n_c, n_s = lax.axis_size("comp"), lax.axis_size("samp")
    c, s = lax.axis_index("comp"), lax.axis_index("samp")
    x, core, z = c % 2, s % 2, s // 2
    n_z = n_s // 2
    z_bits = [1 << i for i in range(n_z.bit_length() - 1)]
    rows, n_local = samples.shape
    width = unmixing.shape[1]
    order = width * n_s
    count = n_local * n_s
    share = width // n_c

    def swap(value, comp_bits=0, samp_bits=0):
        pairs = [
            (i * n_s + j, (i ^ comp_bits) * n_s + (j ^ samp_bits))
            for i in range(n_c)
            for j in range(n_s)
        ]
        return lax.ppermute(value, AXES, pairs)

    def gather_z(piece, bits):
        found = {0: piece}
        for bit in bits:
            found |= {dz ^ bit: swap(p, samp_bits=2 * bit) for dz, p in found.items()}
        return [found[dz] for dz in range(n_z)]

    lower = rows // 2
    own_half = lax.dynamic_slice_in_dim(unmixing, core * lower, lower, 0)
    other_half = lax.dynamic_slice_in_dim(unmixing, (1 - core) * lower, lower, 0)
    other_half = swap(other_half, samp_bits=1)
    own_half = jnp.where(
        core == 0,
        jnp.concatenate([own_half, other_half], axis=1),
        jnp.concatenate([other_half, own_half], axis=1),
    )
    near_half = swap(own_half, comp_bits=1)

    half = n_local // 2
    size = half // CHUNKS
    chunks = [[None] * n_c for _ in range(CHUNKS)]
    for j, pieces in enumerate(chunks):
        sent = lax.dynamic_slice_in_dim(samples, (1 - x) * half + j * size, size, 1)
        pieces[1] = swap(sent, comp_bits=1)
        pieces[0] = lax.dynamic_slice_in_dim(samples, x * half + j * size, size, 1)
        for r in range(2, n_c, 2):
            pieces[r] = swap(pieces[0], comp_bits=r)
        for r in range(2, n_c, 2):
            pieces[r + 1] = swap(pieces[1], comp_bits=r)

    w_own = gather_z(own_half, z_bits)
    w_pieces = w_own + gather_z(near_half, z_bits[::-1])
    wh, wl = assemble_weights(w_pieces, n_z)

    state = None
    for pieces in chunks:
        both = []
        for r in range(n_c):
            both += [pieces[r], swap(pieces[r], samp_bits=1)]
        state = moment_chunk(both, wh, wl, state)
    moment, slope = state

    slope = jnp.sum(slope, axis=1).reshape(2, lower)
    slope = slope + swap(slope, comp_bits=1)[::-1]
    for bit in z_bits:
        slope = slope + swap(slope, samp_bits=2 * bit)

    def halve_comp(value):
        return value[0] + swap(value[1], comp_bits=1)

    def halve_z(value, bit):
        side, axis = (z // bit) % 2, value.ndim - 2
        size = value.shape[axis] // 2
        mine = lax.dynamic_slice_in_dim(value, side * size, size, axis)
        sent = lax.dynamic_slice_in_dim(value, (1 - side) * size, size, axis)
        return mine + swap(sent, samp_bits=2 * bit)

    moment = moment.reshape(2, lower, order)
    front, back = moment[:, :, : order // 2], moment[:, :, order // 2 :]
    front, back = halve_comp(front), halve_z(back, z_bits[0])
    front, back = halve_z(front, z_bits[0]), halve_comp(back)
    for bit in z_bits[1:]:
        front, back = halve_z(front, bit), halve_z(back, bit)
    moment = jnp.concatenate([front, back], axis=1)

    size = moment.shape[0]
    start, span = 0, lower
    for bit in z_bits:
        span //= 2
        start = start + ((z // bit) % 2) * span
    own_slope = lax.dynamic_slice_in_dim(slope[0], start, size, 0) / count
    own_rows = [lax.dynamic_slice_in_dim(p, start, size, 0) for p in w_own]
    for bit in z_bits:
        own_rows = [
            jnp.where((z // bit) % 2 == 0, own_rows[i], own_rows[i ^ bit]) for i in range(n_z)
        ]
    updated = moment / count - own_slope[:, None] * jnp.concatenate(own_rows, axis=1)

    c_bits = [1 << i for i in range(n_c.bit_length() - 1)]
    rows_of = {(0, 0): updated}
    for bit in z_bits[::-1]:
        for dz, _ in list(rows_of):
            rows_of[dz ^ bit, 0] = swap(rows_of[dz, 0], samp_bits=2 * bit)
    for dz in range(n_z):
        for bit in c_bits if dz % 2 else c_bits[::-1]:
            for r in [r for d, r in list(rows_of) if d == dz]:
                rows_of[dz, r ^ bit] = swap(rows_of[dz, r], comp_bits=bit)
    pieces, places = [], []
    for dz, r in spread(n_z, n_c):
        pieces += [rows_of[dz, r], swap(rows_of[dz, r], samp_bits=1)]
        places += [(r, dz, 0), (r, dz, 1)]

    current = newton(pieces, tuple(places), rows, share)

    got = [current[:, :rows]]
    got += [swap(current[:, r * rows : (r + 1) * rows], comp_bits=r) for r in range(1, n_c)]
    bit = 1
    while bit < n_c:
        got = [jnp.where((c // bit) % 2 == 0, got[i], got[i ^ bit]) for i in range(n_c)]
        bit *= 2
    return jnp.concatenate(got, axis=0).T


def solution(mesh):
    return jax.shard_map(
        on_device,
        mesh=mesh,
        in_specs=(P("comp", "samp"), P("comp", "samp")),
        out_specs=P("comp", "samp"),
        check_vma=False,
    )
```

```python
import functools

import jax
import jax.numpy as jnp
from jax import lax
from jax.experimental import pallas as pl
from jax.experimental.pallas import tpu as pltpu
from jax.sharding import PartitionSpec as P


NS_STEPS = 3
AXES = ("comp", "samp")
PARTS = (2, 2, 2, 1, 1)
CHUNKS = len(PARTS)
BLOCKS = 2
LANES = 128
VMEM_BYTES = 60 * 2**20
f32, bf16 = jnp.float32, jnp.bfloat16


def split(v):
    hi = v.astype(bf16)
    return hi, (v - hi.astype(f32)).astype(bf16)


def dot(a, b):
    return jnp.dot(a, b, preferred_element_type=f32)


def dot_nt(a, b):
    return lax.dot_general(a, b, (((1,), (1,)), ((), ())), preferred_element_type=f32)


def weights_kernel(n_z, *refs):
    pieces, (wh, wl) = refs[:-2], refs[-2:]
    z = lax.axis_index("samp") // 2
    rows, width = pieces[0].shape
    for r in range(2):
        for dz in range(n_z):
            hi, lo = split(pieces[r * n_z + dz][...])
            col = pl.multiple_of((z ^ dz) * width, width)
            wh[r * rows : (r + 1) * rows, pl.ds(col, width)] = hi
            wl[r * rows : (r + 1) * rows, pl.ds(col, width)] = lo


def assemble_weights(pieces, n_z):
    rows, width = pieces[0].shape
    shape = jax.ShapeDtypeStruct((2 * rows, n_z * width), bf16)
    return pl.pallas_call(
        functools.partial(weights_kernel, n_z),
        out_shape=(shape, shape),
        in_specs=[pl.BlockSpec(memory_space=pltpu.VMEM)] * len(pieces),
        out_specs=(pl.BlockSpec(memory_space=pltpu.VMEM),) * 2,
        compiler_params=pltpu.CompilerParams(vmem_limit_bytes=VMEM_BYTES),
        cost_estimate=pl.CostEstimate(
            flops=4 * rows * width * len(pieces),
            transcendentals=0,
            bytes_accessed=8 * rows * width * len(pieces),
        ),
    )(*pieces)


def moment_kernel(first, n_p, *refs):
    pieces, refs = refs[:n_p], refs[n_p:]
    if first:
        wh, wl, m_out, s_out, xh, xl = refs
    else:
        wh, wl, m_in, s_in, m_out, s_out, xh, xl = refs
    rows, size = pieces[0].shape
    c = lax.axis_index("comp")

    @pl.when(pl.program_id(0) == 0)
    def _():
        for i, piece in enumerate(pieces):
            hi, lo = split(piece[...])
            place = pl.ds(pl.multiple_of((c ^ (i // 2)) * rows, rows), rows)
            cols = slice(i % 2 * size, (i % 2 + 1) * size)
            xh[place, cols] = hi
            xl[place, cols] = lo

    t = jnp.tanh(dot(wh[...], xh[...]) + dot(wh[...], xl[...]) + dot(wl[...], xh[...]))
    d = 1.0 - t * t
    part = d[:, :LANES]
    for q in range(1, d.shape[1] // LANES):
        part = part + d[:, q * LANES : (q + 1) * LANES]
    s_out[...] = part if first else s_in[...] + part
    th, tl = split(t)
    m = dot_nt(th, xh[...]) + dot_nt(th, xl[...]) + dot_nt(tl, xh[...])
    m_out[...] = m if first else m_in[...] + m


def moment_chunk(pieces, wh, wl, state):
    n_rows, order = wh.shape
    rows, size = pieces[0].shape
    block = n_rows // BLOCKS
    first = state is None
    carried = [] if first else list(state)
    n_p = len(pieces)

    def by_rows(n):
        return pl.BlockSpec((block, n), lambda i: (i, 0))

    once = pl.BlockSpec((rows, size), lambda i: (0, 0), pipeline_mode=pl.Buffered(1))
    return pl.pallas_call(
        functools.partial(moment_kernel, first, n_p),
        grid=(BLOCKS,),
        out_shape=(
            jax.ShapeDtypeStruct((n_rows, order), f32),
            jax.ShapeDtypeStruct((n_rows, LANES), f32),
        ),
        in_specs=[once] * n_p
        + [by_rows(order)] * 2
        + ([] if first else [by_rows(order), by_rows(LANES)]),
        out_specs=(by_rows(order), by_rows(LANES)),
        scratch_shapes=[pltpu.VMEM((order, 2 * size), bf16)] * 2,
        input_output_aliases={} if first else {n_p + 2: 0, n_p + 3: 1},
        compiler_params=pltpu.CompilerParams(
            vmem_limit_bytes=VMEM_BYTES, dimension_semantics=("arbitrary",)
        ),
        cost_estimate=pl.CostEstimate(
            flops=24 * n_rows * order * size,
            transcendentals=2 * n_rows * size,
            bytes_accessed=8 * order * size + 12 * n_rows * order,
        ),
    )(*pieces, wh, wl, *carried)


def schedule(steps):
    products = []

    def advance(level, src, held):
        held = held | {src}
        inner = src
        for k in reversed(range(level)):
            for _ in range(2):
                inner = advance(k, inner, held)
        into = min(set(range(8)) - held - {inner})
        products.append((into, inner, src))
        return into

    value = 0
    for level in range(steps):
        value = advance(level, value, frozenset())
    return products, value


def newton_kernel(last, block, rows, places, n_in, *refs):
    table, pieces, out_ref = refs[0], refs[1 : n_in + 1], refs[n_in + 1]
    stage, uh, ul, gh, gl, rhs, vectors, squares, sem = refs[n_in + 2 :]
    order = uh.shape[0]
    tall, lanes = rhs.shape[0], rhs.shape[0] // 2
    size = pieces[0].shape[0]
    n = order // block
    c, s = lax.axis_index("comp"), lax.axis_index("samp")
    z, core = s // 2, s % 2
    first = (s * (lax.axis_size("comp") * lanes)) + c * lanes
    aligned = pl.multiple_of(first // LANES * LANES, LANES)
    shift = lax.rem(LANES - (first - aligned), LANES)
    slots = stage.shape[0]

    def copy(i):
        return pltpu.make_async_copy(pieces[i], stage.at[i % slots], sem.at[i % slots])

    for i in range(slots - 1):
        copy(i).start()
    squares[...] = jnp.zeros_like(squares)
    for i in range(n_in):
        if i + slots - 1 < n_in:
            copy(i + slots - 1).start()
        copy(i).wait()
        r, dz, dk = places[i]
        start = (core ^ dk) * (rows // 2)
        span, bit = rows // 2, 1
        while span > size:
            span //= 2
            start = start + (((z ^ dz) // bit) % 2) * span
            bit *= 2
        start = r * rows + start

        @pl.loop(0, size // 16)
        def _(q):
            here = pl.ds(pl.multiple_of(start + q * 16, 16), 16)
            v = stage[i % slots, pl.ds(pl.multiple_of(q * 16, 16), 16), :]
            part = v * v
            total = part[:, :LANES]
            for t in range(1, order // LANES):
                total = total + part[:, t * LANES : (t + 1) * LANES]
            squares[...] += total
            hi, lo = split(v)
            uh[here, :] = hi
            ul[here, :] = lo

    @pl.loop(0, order // block)
    def _(b):
        here = pl.ds(pl.multiple_of(b * block, block), block)
        cols = pl.ds(aligned, LANES)
        v = uh[here, cols].astype(f32) + ul[here, cols].astype(f32)
        v = pltpu.roll(v, shift, 1).T[:lanes]
        vectors[0, :lanes, here] = v
        vectors[0, lanes:, here] = v

    @pl.loop(0, n)
    def _(i):
        here = pl.ds(pl.multiple_of(i * block, block), block)

        @pl.loop(0, i + 1)
        def _(j):
            there = pl.ds(pl.multiple_of(j * block, block), block)
            g = dot_nt(uh[here, :], uh[there, :])
            g += dot_nt(uh[here, :], ul[there, :])
            g += dot_nt(ul[here, :], uh[there, :])
            hi, lo = split(g)
            gh[here, there] = hi
            gl[here, there] = lo

            @pl.when(j < i)
            def _():
                hi, lo = split(g.T)
                gh[there, here] = hi
                gl[there, here] = lo

    scale2 = 6.25 * (jnp.sum(squares[...]) / order + 1e-06)
    upper = lax.broadcasted_iota(jnp.int32, (tall, order), 0) < lanes
    tile = order // 2

    @pl.loop(0, table.shape[0] // 3)
    def _(p):
        into, src, base = table[3 * p], table[3 * p + 1], table[3 * p + 2]
        hi, lo = split(vectors[src])
        rhs[...] = jnp.where(upper, hi, lo)

        @pl.loop(0, order // tile)
        def _(b):
            cols = pl.ds(pl.multiple_of(b * tile, tile), tile)
            e = dot(rhs[...], gh[:, cols]) + dot(rhs[...], gl[:, cols])
            e = e + jnp.concatenate([e[lanes:], e[:lanes]], axis=0)
            vectors[into, :, cols] = 1.5 * vectors[base, :, cols] - (0.5 / scale2) * e

    out_ref[...] = vectors[last, :lanes] * (jnp.sqrt(jnp.float32(order)) / jnp.sqrt(scale2))


def newton(pieces, places, rows, share):
    size, order = pieces[0].shape
    block = min(256, order)
    square = pltpu.VMEM((order, order), bf16)
    products, last = schedule(NS_STEPS)
    n_buffers = 1 + max(into for into, _, _ in products)
    table = jnp.array([i for p in products for i in p], jnp.int32)
    return pl.pallas_call(
        functools.partial(newton_kernel, last, block, rows, places, len(pieces)),
        out_shape=jax.ShapeDtypeStruct((share, order), f32),
        in_specs=[pl.BlockSpec(memory_space=pltpu.SMEM)]
        + [pl.BlockSpec(memory_space=pl.ANY)] * len(pieces),
        out_specs=pl.BlockSpec(memory_space=pltpu.VMEM),
        scratch_shapes=[pltpu.VMEM((4, size, order), f32)]
        + [square] * 4
        + [
            pltpu.VMEM((2 * share, order), bf16),
            pltpu.VMEM((n_buffers, 2 * share, order), f32),
            pltpu.VMEM((16, LANES), f32),
            pltpu.SemaphoreType.DMA((4,)),
        ],
        compiler_params=pltpu.CompilerParams(vmem_limit_bytes=VMEM_BYTES),
    )(table, *pieces)


def spread(n_z, n_c):
    every = [(dz, r) for dz in range(n_z) for r in range(n_c)]
    return sorted(every, key=lambda p: (p[0].bit_count() + p[1].bit_count(), p[1], p[0]))


def on_device(samples, unmixing):
    n_c, n_s = lax.axis_size("comp"), lax.axis_size("samp")
    c, s = lax.axis_index("comp"), lax.axis_index("samp")
    x, core, z = c % 2, s % 2, s // 2
    n_z = n_s // 2
    z_bits = [1 << i for i in range(n_z.bit_length() - 1)]
    rows, n_local = samples.shape
    width = unmixing.shape[1]
    order = width * n_s
    count = n_local * n_s
    share = width // n_c

    def swap(value, comp_bits=0, samp_bits=0):
        pairs = [
            (i * n_s + j, (i ^ comp_bits) * n_s + (j ^ samp_bits))
            for i in range(n_c)
            for j in range(n_s)
        ]
        return lax.ppermute(value, AXES, pairs)

    def gather_z(piece, bits):
        found = {0: piece}
        for bit in bits:
            found |= {dz ^ bit: swap(p, samp_bits=2 * bit) for dz, p in found.items()}
        return [found[dz] for dz in range(n_z)]

    lower = rows // 2
    own_half = lax.dynamic_slice_in_dim(unmixing, core * lower, lower, 0)
    other_half = lax.dynamic_slice_in_dim(unmixing, (1 - core) * lower, lower, 0)
    other_half = swap(other_half, samp_bits=1)
    own_half = jnp.where(
        core == 0,
        jnp.concatenate([own_half, other_half], axis=1),
        jnp.concatenate([other_half, own_half], axis=1),
    )
    near_half = swap(own_half, comp_bits=1)

    half = n_local // 2
    unit = half // sum(PARTS)
    chunks = [[None] * n_c for _ in range(CHUNKS)]
    for j, pieces in enumerate(chunks):
        size, offset = PARTS[j] * unit, sum(PARTS[:j]) * unit
        sent = lax.dynamic_slice_in_dim(samples, (1 - x) * half + offset, size, 1)
        pieces[1] = swap(sent, comp_bits=1)
        pieces[0] = lax.dynamic_slice_in_dim(samples, x * half + offset, size, 1)
        for r in range(2, n_c, 2):
            pieces[r] = swap(pieces[0], comp_bits=r)
        for r in range(2, n_c, 2):
            pieces[r + 1] = swap(pieces[1], comp_bits=r)

    w_own = gather_z(own_half, z_bits)
    w_pieces = w_own + gather_z(near_half, z_bits[::-1])
    wh, wl = assemble_weights(w_pieces, n_z)

    state = None
    for pieces in chunks:
        both = []
        for r in range(n_c):
            both += [pieces[r], swap(pieces[r], samp_bits=1)]
        state = moment_chunk(both, wh, wl, state)
    moment, slope = state

    slope = jnp.sum(slope, axis=1).reshape(2, lower)
    slope = slope + swap(slope, comp_bits=1)[::-1]
    for bit in z_bits:
        slope = slope + swap(slope, samp_bits=2 * bit)

    def halve_comp(value):
        return value[0] + swap(value[1], comp_bits=1)

    def halve_z(value, bit):
        side, axis = (z // bit) % 2, value.ndim - 2
        size = value.shape[axis] // 2
        mine = lax.dynamic_slice_in_dim(value, side * size, size, axis)
        sent = lax.dynamic_slice_in_dim(value, (1 - side) * size, size, axis)
        return mine + swap(sent, samp_bits=2 * bit)

    moment = moment.reshape(2, lower, order)
    front, back = moment[:, :, : order // 2], moment[:, :, order // 2 :]
    front, back = halve_comp(front), halve_z(back, z_bits[0])
    front, back = halve_z(front, z_bits[0]), halve_comp(back)
    for bit in z_bits[1:]:
        front, back = halve_z(front, bit), halve_z(back, bit)
    moment = jnp.concatenate([front, back], axis=1)

    size = moment.shape[0]
    start, span = 0, lower
    for bit in z_bits:
        span //= 2
        start = start + ((z // bit) % 2) * span
    own_slope = lax.dynamic_slice_in_dim(slope[0], start, size, 0) / count
    own_rows = [lax.dynamic_slice_in_dim(p, start, size, 0) for p in w_own]
    for bit in z_bits:
        own_rows = [
            jnp.where((z // bit) % 2 == 0, own_rows[i], own_rows[i ^ bit]) for i in range(n_z)
        ]
    updated = moment / count - own_slope[:, None] * jnp.concatenate(own_rows, axis=1)

    c_bits = [1 << i for i in range(n_c.bit_length() - 1)]
    rows_of = {(0, 0): updated}
    for bit in z_bits[::-1]:
        for dz, _ in list(rows_of):
            rows_of[dz ^ bit, 0] = swap(rows_of[dz, 0], samp_bits=2 * bit)
    for dz in range(n_z):
        for bit in c_bits if dz % 2 else c_bits[::-1]:
            for r in [r for d, r in list(rows_of) if d == dz]:
                rows_of[dz, r ^ bit] = swap(rows_of[dz, r], comp_bits=bit)
    pieces, places = [], []
    for dz, r in spread(n_z, n_c):
        pieces += [rows_of[dz, r], swap(rows_of[dz, r], samp_bits=1)]
        places += [(r, dz, 0), (r, dz, 1)]

    current = newton(pieces, tuple(places), rows, share)

    got = [current[:, :rows]]
    got += [swap(current[:, r * rows : (r + 1) * rows], comp_bits=r) for r in range(1, n_c)]
    bit = 1
    while bit < n_c:
        got = [jnp.where((c // bit) % 2 == 0, got[i], got[i ^ bit]) for i in range(n_c)]
        bit *= 2
    return jnp.concatenate(got, axis=0).T


def solution(mesh):
    return jax.shard_map(
        on_device,
        mesh=mesh,
        in_specs=(P("comp", "samp"), P("comp", "samp")),
        out_specs=P("comp", "samp"),
        check_vma=False,
    )
```

```python
import functools

import jax
import jax.numpy as jnp
from jax import lax
from jax.experimental import pallas as pl
from jax.experimental.pallas import tpu as pltpu
from jax.sharding import PartitionSpec as P


NS_STEPS = 3
AXES = ("comp", "samp")
PARTS = (2, 2, 2, 1, 1)
CHUNKS = len(PARTS)
BLOCKS = 4
LANES = 128
VMEM_BYTES = 60 * 2**20
f32, bf16 = jnp.float32, jnp.bfloat16


def split(v):
    hi = v.astype(bf16)
    return hi, (v - hi.astype(f32)).astype(bf16)


def dot(a, b):
    return jnp.dot(a, b, preferred_element_type=f32)


def dot_nt(a, b):
    return lax.dot_general(a, b, (((1,), (1,)), ((), ())), preferred_element_type=f32)


def weights_kernel(n_z, *refs):
    pieces, (wh, wl) = refs[:-2], refs[-2:]
    z = lax.axis_index("samp") // 2
    rows, width = pieces[0].shape
    for r in range(2):
        for dz in range(n_z):
            hi, lo = split(pieces[r * n_z + dz][...])
            col = pl.multiple_of((z ^ dz) * width, width)
            wh[r * rows : (r + 1) * rows, pl.ds(col, width)] = hi
            wl[r * rows : (r + 1) * rows, pl.ds(col, width)] = lo


def assemble_weights(pieces, n_z):
    rows, width = pieces[0].shape
    shape = jax.ShapeDtypeStruct((2 * rows, n_z * width), bf16)
    return pl.pallas_call(
        functools.partial(weights_kernel, n_z),
        out_shape=(shape, shape),
        in_specs=[pl.BlockSpec(memory_space=pltpu.VMEM)] * len(pieces),
        out_specs=(pl.BlockSpec(memory_space=pltpu.VMEM),) * 2,
        compiler_params=pltpu.CompilerParams(vmem_limit_bytes=VMEM_BYTES),
        cost_estimate=pl.CostEstimate(
            flops=4 * rows * width * len(pieces),
            transcendentals=0,
            bytes_accessed=8 * rows * width * len(pieces),
        ),
    )(*pieces)


def moment_kernel(first, n_p, *refs):
    pieces, refs = refs[:n_p], refs[n_p:]
    if first:
        wh, wl, m_out, s_out, xh, xl = refs
    else:
        wh, wl, m_in, s_in, m_out, s_out, xh, xl = refs
    rows, size = pieces[0].shape
    c = lax.axis_index("comp")

    @pl.when(pl.program_id(0) == 0)
    def _():
        for i, piece in enumerate(pieces):
            hi, lo = split(piece[...])
            place = pl.ds(pl.multiple_of((c ^ (i // 2)) * rows, rows), rows)
            cols = slice(i % 2 * size, (i % 2 + 1) * size)
            xh[place, cols] = hi
            xl[place, cols] = lo

    t = jnp.tanh(dot(wh[...], xh[...]) + dot(wh[...], xl[...]) + dot(wl[...], xh[...]))
    d = 1.0 - t * t
    part = d[:, :LANES]
    for q in range(1, d.shape[1] // LANES):
        part = part + d[:, q * LANES : (q + 1) * LANES]
    s_out[...] = part if first else s_in[...] + part
    th, tl = split(t)
    m = dot_nt(th, xh[...]) + dot_nt(th, xl[...]) + dot_nt(tl, xh[...])
    m_out[...] = m if first else m_in[...] + m


def moment_chunk(pieces, wh, wl, state):
    n_rows, order = wh.shape
    rows, size = pieces[0].shape
    block = n_rows // BLOCKS
    first = state is None
    carried = [] if first else list(state)
    n_p = len(pieces)

    def by_rows(n):
        return pl.BlockSpec((block, n), lambda i: (i, 0))

    once = pl.BlockSpec((rows, size), lambda i: (0, 0), pipeline_mode=pl.Buffered(1))
    return pl.pallas_call(
        functools.partial(moment_kernel, first, n_p),
        grid=(BLOCKS,),
        out_shape=(
            jax.ShapeDtypeStruct((n_rows, order), f32),
            jax.ShapeDtypeStruct((n_rows, LANES), f32),
        ),
        in_specs=[once] * n_p
        + [by_rows(order)] * 2
        + ([] if first else [by_rows(order), by_rows(LANES)]),
        out_specs=(by_rows(order), by_rows(LANES)),
        scratch_shapes=[pltpu.VMEM((order, 2 * size), bf16)] * 2,
        input_output_aliases={} if first else {n_p + 2: 0, n_p + 3: 1},
        compiler_params=pltpu.CompilerParams(
            vmem_limit_bytes=VMEM_BYTES, dimension_semantics=("arbitrary",)
        ),
        cost_estimate=pl.CostEstimate(
            flops=24 * n_rows * order * size,
            transcendentals=2 * n_rows * size,
            bytes_accessed=8 * order * size + 12 * n_rows * order,
        ),
    )(*pieces, wh, wl, *carried)


def schedule(steps):
    products = []

    def advance(level, src, held):
        held = held | {src}
        inner = src
        for k in reversed(range(level)):
            for _ in range(2):
                inner = advance(k, inner, held)
        into = min(set(range(8)) - held - {inner})
        products.append((into, inner, src))
        return into

    value = 0
    for level in range(steps):
        value = advance(level, value, frozenset())
    return products, value


def newton_kernel(last, block, rows, places, n_in, *refs):
    table, pieces, out_ref = refs[0], refs[1 : n_in + 1], refs[n_in + 1]
    stage, uh, ul, gh, gl, rhs, vectors, squares, sem = refs[n_in + 2 :]
    order = uh.shape[0]
    tall, lanes = rhs.shape[0], rhs.shape[0] // 2
    size = pieces[0].shape[0]
    n = order // block
    c, s = lax.axis_index("comp"), lax.axis_index("samp")
    z, core = s // 2, s % 2
    first = (s * (lax.axis_size("comp") * lanes)) + c * lanes
    aligned = pl.multiple_of(first // LANES * LANES, LANES)
    shift = lax.rem(LANES - (first - aligned), LANES)
    slots = stage.shape[0]

    def copy(i):
        return pltpu.make_async_copy(pieces[i], stage.at[i % slots], sem.at[i % slots])

    for i in range(slots - 1):
        copy(i).start()
    squares[...] = jnp.zeros_like(squares)
    for i in range(n_in):
        if i + slots - 1 < n_in:
            copy(i + slots - 1).start()
        copy(i).wait()
        r, dz, dk = places[i]
        start = (core ^ dk) * (rows // 2)
        span, bit = rows // 2, 1
        while span > size:
            span //= 2
            start = start + (((z ^ dz) // bit) % 2) * span
            bit *= 2
        start = r * rows + start

        part_cols = order // 4

        @pl.loop(0, size // 16 * 4)
        def _(q):
            row, cols = q // 4 * 16, pl.ds(pl.multiple_of(q % 4 * part_cols, part_cols), part_cols)
            here = pl.ds(pl.multiple_of(start + row, 16), 16)
            v = stage[i % slots, pl.ds(pl.multiple_of(row, 16), 16), cols]
            part = v * v
            total = part[:, :LANES]
            for t in range(1, part_cols // LANES):
                total = total + part[:, t * LANES : (t + 1) * LANES]
            squares[...] += total
            hi, lo = split(v)
            uh[here, cols] = hi
            ul[here, cols] = lo

    @pl.loop(0, order // block)
    def _(b):
        here = pl.ds(pl.multiple_of(b * block, block), block)
        cols = pl.ds(aligned, LANES)
        v = uh[here, cols].astype(f32) + ul[here, cols].astype(f32)
        v = pltpu.roll(v, shift, 1).T[:lanes]
        vectors[0, :lanes, here] = v
        vectors[0, lanes:, here] = v

    @pl.loop(0, n)
    def _(i):
        here = pl.ds(pl.multiple_of(i * block, block), block)

        @pl.loop(0, i + 1)
        def _(j):
            there = pl.ds(pl.multiple_of(j * block, block), block)
            g = dot_nt(uh[here, :], uh[there, :])
            g += dot_nt(uh[here, :], ul[there, :])
            g += dot_nt(ul[here, :], uh[there, :])
            hi, lo = split(g)
            gh[here, there] = hi
            gl[here, there] = lo

            @pl.when(j < i)
            def _():
                hi, lo = split(g.T)
                gh[there, here] = hi
                gl[there, here] = lo

    scale2 = 6.25 * (jnp.sum(squares[...]) / order + 1e-06)
    upper = lax.broadcasted_iota(jnp.int32, (tall, order), 0) < lanes
    tile = order // 2

    @pl.loop(0, table.shape[0] // 3)
    def _(p):
        into, src, base = table[3 * p], table[3 * p + 1], table[3 * p + 2]
        hi, lo = split(vectors[src])
        rhs[...] = jnp.where(upper, hi, lo)

        @pl.loop(0, order // tile)
        def _(b):
            cols = pl.ds(pl.multiple_of(b * tile, tile), tile)
            e = dot(rhs[...], gh[:, cols]) + dot(rhs[...], gl[:, cols])
            e = e + jnp.concatenate([e[lanes:], e[:lanes]], axis=0)
            vectors[into, :, cols] = 1.5 * vectors[base, :, cols] - (0.5 / scale2) * e

    out_ref[...] = vectors[last, :lanes] * (jnp.sqrt(jnp.float32(order)) / jnp.sqrt(scale2))


def newton(pieces, places, rows, share):
    size, order = pieces[0].shape
    block = min(256, order)
    square = pltpu.VMEM((order, order), bf16)
    products, last = schedule(NS_STEPS)
    n_buffers = 1 + max(into for into, _, _ in products)
    table = jnp.array([i for p in products for i in p], jnp.int32)
    return pl.pallas_call(
        functools.partial(newton_kernel, last, block, rows, places, len(pieces)),
        out_shape=jax.ShapeDtypeStruct((share, order), f32),
        in_specs=[pl.BlockSpec(memory_space=pltpu.SMEM)]
        + [pl.BlockSpec(memory_space=pl.ANY)] * len(pieces),
        out_specs=pl.BlockSpec(memory_space=pltpu.VMEM),
        scratch_shapes=[pltpu.VMEM((4, size, order), f32)]
        + [square] * 4
        + [
            pltpu.VMEM((2 * share, order), bf16),
            pltpu.VMEM((n_buffers, 2 * share, order), f32),
            pltpu.VMEM((16, LANES), f32),
            pltpu.SemaphoreType.DMA((4,)),
        ],
        compiler_params=pltpu.CompilerParams(vmem_limit_bytes=VMEM_BYTES),
    )(table, *pieces)


def spread(n_z, n_c):
    every = [(dz, r) for dz in range(n_z) for r in range(n_c)]
    return sorted(every, key=lambda p: (p[0].bit_count() + p[1].bit_count(), p[1], p[0]))


def on_device(samples, unmixing):
    n_c, n_s = lax.axis_size("comp"), lax.axis_size("samp")
    c, s = lax.axis_index("comp"), lax.axis_index("samp")
    x, core, z = c % 2, s % 2, s // 2
    n_z = n_s // 2
    z_bits = [1 << i for i in range(n_z.bit_length() - 1)]
    rows, n_local = samples.shape
    width = unmixing.shape[1]
    order = width * n_s
    count = n_local * n_s
    share = width // n_c

    def swap(value, comp_bits=0, samp_bits=0):
        pairs = [
            (i * n_s + j, (i ^ comp_bits) * n_s + (j ^ samp_bits))
            for i in range(n_c)
            for j in range(n_s)
        ]
        return lax.ppermute(value, AXES, pairs)

    def gather_z(piece, bits):
        found = {0: piece}
        for bit in bits:
            found |= {dz ^ bit: swap(p, samp_bits=2 * bit) for dz, p in found.items()}
        return [found[dz] for dz in range(n_z)]

    lower = rows // 2
    own_half = lax.dynamic_slice_in_dim(unmixing, core * lower, lower, 0)
    other_half = lax.dynamic_slice_in_dim(unmixing, (1 - core) * lower, lower, 0)
    other_half = swap(other_half, samp_bits=1)
    own_half = jnp.where(
        core == 0,
        jnp.concatenate([own_half, other_half], axis=1),
        jnp.concatenate([other_half, own_half], axis=1),
    )
    near_half = swap(own_half, comp_bits=1)

    half = n_local // 2
    unit = half // sum(PARTS)
    chunks = [[None] * n_c for _ in range(CHUNKS)]
    for j, pieces in enumerate(chunks):
        size, offset = PARTS[j] * unit, sum(PARTS[:j]) * unit
        sent = lax.dynamic_slice_in_dim(samples, (1 - x) * half + offset, size, 1)
        pieces[1] = swap(sent, comp_bits=1)
        pieces[0] = lax.dynamic_slice_in_dim(samples, x * half + offset, size, 1)
        for r in range(2, n_c, 2):
            pieces[r] = swap(pieces[0], comp_bits=r)
        for r in range(2, n_c, 2):
            pieces[r + 1] = swap(pieces[1], comp_bits=r)

    w_own = gather_z(own_half, z_bits)
    w_pieces = w_own + gather_z(near_half, z_bits[::-1])
    wh, wl = assemble_weights(w_pieces, n_z)

    state = None
    for pieces in chunks:
        both = []
        for r in range(n_c):
            both += [pieces[r], swap(pieces[r], samp_bits=1)]
        state = moment_chunk(both, wh, wl, state)
    moment, slope = state

    slope = jnp.sum(slope, axis=1).reshape(2, lower)
    slope = slope + swap(slope, comp_bits=1)[::-1]
    for bit in z_bits:
        slope = slope + swap(slope, samp_bits=2 * bit)

    def halve_comp(value):
        return value[0] + swap(value[1], comp_bits=1)

    def halve_z(value, bit):
        side, axis = (z // bit) % 2, value.ndim - 2
        size = value.shape[axis] // 2
        mine = lax.dynamic_slice_in_dim(value, side * size, size, axis)
        sent = lax.dynamic_slice_in_dim(value, (1 - side) * size, size, axis)
        return mine + swap(sent, samp_bits=2 * bit)

    moment = moment.reshape(2, lower, order)
    front, back = moment[:, :, : order // 2], moment[:, :, order // 2 :]
    front, back = halve_comp(front), halve_z(back, z_bits[0])
    front, back = halve_z(front, z_bits[0]), halve_comp(back)
    for bit in z_bits[1:]:
        front, back = halve_z(front, bit), halve_z(back, bit)
    moment = jnp.concatenate([front, back], axis=1)

    size = moment.shape[0]
    start, span = 0, lower
    for bit in z_bits:
        span //= 2
        start = start + ((z // bit) % 2) * span
    own_slope = lax.dynamic_slice_in_dim(slope[0], start, size, 0) / count
    own_rows = [lax.dynamic_slice_in_dim(p, start, size, 0) for p in w_own]
    for bit in z_bits:
        own_rows = [
            jnp.where((z // bit) % 2 == 0, own_rows[i], own_rows[i ^ bit]) for i in range(n_z)
        ]
    updated = moment / count - own_slope[:, None] * jnp.concatenate(own_rows, axis=1)

    c_bits = [1 << i for i in range(n_c.bit_length() - 1)]
    rows_of = {(0, 0): updated}
    for bit in z_bits[::-1]:
        for dz, _ in list(rows_of):
            rows_of[dz ^ bit, 0] = swap(rows_of[dz, 0], samp_bits=2 * bit)
    for dz in range(n_z):
        for bit in c_bits if dz % 2 else c_bits[::-1]:
            for r in [r for d, r in list(rows_of) if d == dz]:
                rows_of[dz, r ^ bit] = swap(rows_of[dz, r], comp_bits=bit)
    pieces, places = [], []
    for dz, r in spread(n_z, n_c):
        pieces += [rows_of[dz, r], swap(rows_of[dz, r], samp_bits=1)]
        places += [(r, dz, 0), (r, dz, 1)]

    current = newton(pieces, tuple(places), rows, share)

    got = [current[:, :rows]]
    got += [swap(current[:, r * rows : (r + 1) * rows], comp_bits=r) for r in range(1, n_c)]
    bit = 1
    while bit < n_c:
        got = [jnp.where((c // bit) % 2 == 0, got[i], got[i ^ bit]) for i in range(n_c)]
        bit *= 2
    return jnp.concatenate(got, axis=0).T


def solution(mesh):
    return jax.shard_map(
        on_device,
        mesh=mesh,
        in_specs=(P("comp", "samp"), P("comp", "samp")),
        out_specs=P("comp", "samp"),
        check_vma=False,
    )
```
